256 devices in a mesh: sub: 256 (over z, y, x, core).
Axes of the slice: x: 4, y: 4, z: 8, core: 2. Of those that a mesh axis runs over, the one named last changes fastest.
Arguments:
- applied_loads: float32 [294912, 128], P('sub'), may hold values from -60 to 60
- local_inverse: float32 [294912, 1152], P('sub'), may hold values from -1 to 2
- schur_block: float32 [294912, 1152], P('sub'), may hold values from -1 to 2
- coarse_modes: float32 [3072, 1152], P('sub'), may hold values from -0.1875 to 0.1875
- coarse_rows: float32 [3072, 3072], P('sub'), may hold values from -1 to 8
- mode_ids: int32 [256, 12], replicated, may hold values from 0 to 3071, as said below
- neighbours: int32 [256, 6], P('sub'), may hold values from -1 to 255, as said below
- iface_rows: int32 [256, 6, 192], P('sub'), may hold values from -1 to 1151, as said below
Outputs:
- multiplier: float32 [294912, 128], P('sub')
- displacement: float32 [294912, 128], P('sub')
The draws below stay inside these ranges and needn't reach their ends.
Inputs may be any that keep to these rules, and one draw needn't show every extreme that they name: neighbours[s, k] is -1 or s + o_k with o = (1, -1, 4, -4, 16, -16) in a grid of 4 x 4 x 16 subdomains numbered with the first dimension fastest; t = neighbours[s, k] >= 0 gives neighbours[t, k xor 1] = s. Each list iface_rows[s, k] holds distinct rows followed by -1; it is all -1 where neighbours[s, k] = -1; the two lists of a face hold equally many rows; some list holds exactly 192 rows. mode_ids holds every mode number once.
All inputs are finite; a program needn't handle non-finite values.
Results may differ from the reference program's by a relative error of at most 0.0003.
Values sent between devices are 32-bit elements; how exact they have to be, the bound alone decides.
A program may use at most 128 MiB of HBM per device.

```python
import math
import jax
import jax.numpy as jnp
from jax import lax

ORDER = 1152
COLS = 128
MODES_SUB = 12
IFACE = 192
ITERS = 3
GRID_X = 4
GRID_Y = 4
MODES = 3072
N_SUB = 256


def interface_layout(key):
    device_id = jnp.arange(N_SUB, dtype=jnp.int32)
    place_x = device_id % GRID_X
    place_y = device_id // GRID_X % GRID_Y
    place_z = device_id // (GRID_X * GRID_Y)
    layers = N_SUB // (GRID_X * GRID_Y)
    inside_up = jnp.stack([place_x + 1 < GRID_X, place_y + 1 < GRID_Y, place_z + 1 < layers], axis=1)
    inside_down = [place_x > 0, place_y > 0, place_z > 0]
    key_live, key_length, key_order = jax.random.split(key, 3)
    alive = jax.random.randint(key_live, (N_SUB, 3), 0, 8) != 0
    alive = alive.at[0, 0].set(True)
    face_live = inside_up & alive
    face_length = jax.random.randint(key_length, (N_SUB, 3), IFACE // 2, IFACE + 1)
    face_length = face_length.at[0, 0].set(IFACE)
    strides = [1, GRID_X, GRID_X * GRID_Y]
    live_columns = []
    length_columns = []
    partner_columns = []
    for axis_id in range(3):
        stride = strides[axis_id]
        live_columns.append(face_live[:, axis_id])
        length_columns.append(face_length[:, axis_id])
        partner_columns.append(device_id + stride)
        owners = jnp.clip(device_id - stride, 0, N_SUB - 1)
        live_columns.append(inside_down[axis_id] & face_live[owners, axis_id])
        length_columns.append(face_length[owners, axis_id])
        partner_columns.append(device_id - stride)
    slot_live = jnp.stack(live_columns, axis=1)
    slot_length = jnp.stack(length_columns, axis=1)
    partner = jnp.stack(partner_columns, axis=1)
    neighbours = jnp.where(slot_live, partner, -1).astype(jnp.int32)
    slot_keys = jax.random.split(key_order, N_SUB * 6)
    shuffled = jax.vmap(lambda slot_key: jax.random.permutation(slot_key, ORDER)[:IFACE])(slot_keys)
    shuffled = shuffled.reshape(N_SUB, 6, IFACE)
    position = jnp.arange(IFACE, dtype=jnp.int32)[None, None, :]
    kept = slot_live[:, :, None] & (position < slot_length[:, :, None])
    row_lists = jnp.where(kept, shuffled, -1).astype(jnp.int32)
    return (neighbours, row_lists)


def draw_neighbours(key, part):
    return interface_layout(jax.random.fold_in(key, 11))[0]


def draw_iface_rows(key, part):
    return interface_layout(jax.random.fold_in(key, 11))[1]


def mode_order(key):
    return jax.random.permutation(jax.random.fold_in(key, 5), MODES).astype(jnp.int32)


def draw_mode_ids(key, part):
    return mode_order(key).reshape(N_SUB, MODES_SUB)


def draw_coarse_rows(key, part):
    order_ids = mode_order(key)
    key_values, key_diagonal = jax.random.split(jax.random.fold_in(key, 6))
    spread = jax.random.truncated_normal(key_values, -4.0, 4.0, (MODES, MODES), jnp.float32)
    identity = jnp.eye(MODES, dtype=jnp.float32)
    spread = spread * (2.0 / math.sqrt(MODES)) * (1.0 - identity)
    diagonal = jax.random.uniform(key_diagonal, (MODES,), jnp.float32, 4.0, 8.0)
    whole = spread + identity * diagonal[None, :]
    return whole[order_ids]


def diagonal_block(key, lowest, highest):
    key_values, key_diagonal = jax.random.split(key)
    spread = jax.random.truncated_normal(key_values, -4.0, 4.0, (N_SUB, ORDER, ORDER), jnp.float32)
    identity = jnp.eye(ORDER, dtype=jnp.float32)[None, :, :]
    spread = spread * (0.5 / math.sqrt(ORDER)) * (1.0 - identity)
    scales = jax.random.uniform(key_diagonal, (N_SUB, ORDER, 1), jnp.float32, lowest, highest)
    return (spread + scales * identity).reshape(N_SUB * ORDER, ORDER)


def draw_local_inverse(key, part):
    return diagonal_block(jax.random.fold_in(key, 1), 1.0, 2.0)


def draw_schur_block(key, part):
    return diagonal_block(jax.random.fold_in(key, 2), 0.5, 1.5)


def draw_applied_loads(key, part):
    key_values, key_scales = jax.random.split(jax.random.fold_in(key, 3), 2)
    device_scale = 1.0 + 2.0 * jnp.arange(N_SUB, dtype=jnp.float32)[:, None, None] / max(N_SUB - 1, 1)
    column_scale = jnp.exp(jax.random.uniform(key_scales, (1, 1, COLS), jnp.float32, -1.15, 1.15))
    values = jax.random.truncated_normal(key_values, -4.0, 4.0, (N_SUB, ORDER, COLS), jnp.float32)
    return (values * device_scale * column_scale).reshape(N_SUB * ORDER, COLS)


def level_of(own_key, shape, cuts, least, top_value):
    factor_of, own = 1.0, jax.random.fold_in(own_key, 6)
    for dim, parts in cuts:
        steps = jnp.exp(jax.random.uniform(jax.random.fold_in(own, dim), (parts,), jnp.float32, least / len(cuts), top_value / len(cuts)))
        factor_of = factor_of * jnp.repeat(steps, shape[dim] // parts).reshape([-1 if axis == dim else 1 for axis in range(len(shape))])
    return factor_of


def noise(stream_key, extent, deviation, reach, cuts=(), kind=jnp.bfloat16):
    drawn = jax.random.normal(stream_key, extent, jnp.float32) * deviation
    if len(cuts) > 0:
        drawn = level_of(stream_key, extent, cuts, -0.22, 0.18) * drawn
    return jnp.clip(drawn, min=-reach, max=reach).astype(kind)


def setup_inputs(seed: int = 0) -> dict:
    splits = jax.random.split(jax.random.key(seed), 9)
    applied_loads = draw_applied_loads(jax.random.fold_in(splits[8], 71), 0)
    local_inverse = draw_local_inverse(jax.random.fold_in(splits[8], 71), 0)
    schur_block = draw_schur_block(jax.random.fold_in(splits[8], 71), 0)
    coarse_modes = noise(splits[3], (N_SUB * MODES_SUB, ORDER), ORDER ** -0.5, 0.1875, ((0, 256),), jnp.float32)
    coarse_rows = draw_coarse_rows(jax.random.fold_in(splits[8], 71), 0)
    mode_ids = draw_mode_ids(jax.random.fold_in(splits[8], 71), 0)
    neighbours = draw_neighbours(jax.random.fold_in(splits[8], 71), 0)
    iface_rows = draw_iface_rows(jax.random.fold_in(splits[8], 71), 0)
    return {"applied_loads": applied_loads, "local_inverse": local_inverse, "schur_block": schur_block, "coarse_modes": coarse_modes, "coarse_rows": coarse_rows, "mode_ids": mode_ids, "neighbours": neighbours, "iface_rows": iface_rows}


DAMPING = 0.8
EPSILON = 1e-6
HIGHEST_PRECISION = lax.Precision.HIGHEST


def jump_of(source_field, neighbours, iface_rows):
    usable = (iface_rows >= 0) & (neighbours >= 0)[:, :, None]
    row_lists = jnp.maximum(iface_rows, 0).astype(jnp.int32)
    partner = jnp.maximum(neighbours, 0).astype(jnp.int32)
    swapped = row_lists[:, jnp.array([1, 0, 3, 2, 5, 4], dtype=jnp.int32), :]
    partner_rows = swapped[partner, jnp.arange(6, dtype=jnp.int32)[None, :]]
    device_ids = jnp.arange(source_field.shape[0], dtype=jnp.int32)[:, None, None]
    own_rows = source_field[device_ids, row_lists]
    other_rows = source_field[partner[:, :, None], partner_rows]
    difference = jnp.where(usable[..., None], own_rows - other_rows, jnp.zeros_like(own_rows))
    return jnp.zeros_like(source_field).at[device_ids, row_lists].add(difference)


def blocks(matrix, operand):
    return jnp.einsum("smk,skr->smr", matrix, operand, precision=HIGHEST_PRECISION)


def reference(applied_loads, local_inverse, schur_block, coarse_modes, coarse_rows, mode_ids, neighbours, iface_rows):
    load_cube = applied_loads.reshape(N_SUB, ORDER, COLS)
    inverse_cube = local_inverse.reshape(N_SUB, ORDER, ORDER)
    schur_cube = schur_block.reshape(N_SUB, ORDER, ORDER)
    mode_cube = coarse_modes.reshape(N_SUB, MODES_SUB, ORDER)
    ordered = jnp.take(coarse_rows, mode_ids.reshape(-1).astype(jnp.int32), axis=1)
    displacement = blocks(inverse_cube, load_cube)
    multiplier = jnp.zeros_like(load_cube)
    residual = jump_of(displacement, neighbours, iface_rows)
    for sweep_id in range(ITERS):
        smoothed = blocks(schur_cube, residual)
        projected = jnp.einsum("sjm,smr->sjr", mode_cube, smoothed, precision=HIGHEST_PRECISION)
        coarse = jnp.dot(ordered, projected.reshape(MODES, COLS), precision=HIGHEST_PRECISION)
        coarse = coarse.reshape(N_SUB, MODES_SUB, COLS)
        direction = smoothed + jnp.einsum("sjm,sjr->smr", mode_cube, coarse, precision=HIGHEST_PRECISION)
        lifted = jump_of(direction, neighbours, iface_rows)
        response = blocks(inverse_cube, lifted)
        image_field = jump_of(response, neighbours, iface_rows)
        numerator = jnp.sum(residual * image_field, axis=(0, 1))
        denominator = jnp.sum(image_field * image_field, axis=(0, 1)) + EPSILON
        step_size = DAMPING * numerator / denominator
        multiplier = multiplier + step_size * direction
        displacement = displacement - step_size * response
        residual = residual - step_size * image_field
    return multiplier.reshape(N_SUB * ORDER, COLS), displacement.reshape(N_SUB * ORDER, COLS)
```

```python
import jax
import jax.numpy as jnp
from jax import lax
from jax.experimental import pallas as pl
from jax.experimental.pallas import tpu as pltpu
from jax.sharding import PartitionSpec as P

ORDER = 1152
COLS = 128
MODES_SUB = 12
IFACE = 192
SLOTS = 6
ITERS = 3
DEVICES = 256
DAMPING = 0.8
EPSILON = 1e-06
OFFSETS = (1, -1, 4, -4, 16, -16)
STRIDES = (1, 4, 16)
EXTENTS = (4, 4, 16)
GROUP = 16
BLK = 16
JUMPS = 2 + 2 * ITERS
ROUNDS = ITERS + 1
TILE = 384
F32 = jnp.float32
BF16 = jnp.bfloat16
MESH = pl.DeviceIdType.MESH
PAIRS = ((2, 3), (4, 5), (0, 1))


def dot(a, b):
    return jnp.dot(a, b, preferred_element_type=F32)


def split(value):
    high = value.astype(BF16)
    low = (value - high.astype(F32)).astype(BF16)
    return high, low


def fold(value):
    return value[:, :COLS] + value[:, COLS:]


def kernel(
    loads_hbm, inverse_hbm, schur_hbm, modes_in, rows_in, ids_in, iface_in,
    mult_hbm, disp_hbm,
    stage_k, stage_s, k_hi, k_lo, s_hi, s_lo, scatter_m, gather_m,
    out_buf, in_buf, vec, vec2, cnt, phi_t, u, w, lifted, rw, smoothed, response, gap, disp, mult, og,
    gw, m_hi, m_lo, em_hi, em_lo, ps, phi_pad, c_pad, c_send, c_recv, cb_hi, cb_lo,
    pbuf, part, rbuf, cst, coarse, mult_co,
    load_sem, out_sem, jump_send, jump_recv, c_ssem, c_rsem, p_ssem, p_rsem, q_ssem, q_rsem, n_ssem, n_rsem,
):
    me = lax.axis_index("sub")
    core = lax.rem(me, 2)
    yx = lax.rem(lax.div(me, 2), GROUP)
    zc = lax.div(me, 32) * 2 + core

    def has(slot):
        axis = slot // 2
        place = lax.rem(lax.div(me, STRIDES[axis]), EXTENTS[axis])
        return place < EXTENTS[axis] - 1 if slot % 2 == 0 else place > 0

    def along_z(index):
        return lax.div(index, 2) * 32 + yx * 2 + lax.rem(index, 2)

    def along_plane(index):
        return lax.div(me, 32) * 32 + index * 2 + core

    copies_k, copies_s = [], []
    load_copy = pltpu.make_async_copy(loads_hbm, disp, load_sem.at[6])
    load_copy.start()
    for i in range(3):
        part_rows = pl.ds(i * TILE, TILE)
        copy = pltpu.make_async_copy(inverse_hbm.at[part_rows], stage_k.at[part_rows], load_sem.at[i])
        copy.start()
        copies_k.append(copy)
    for i in range(3):
        part_rows = pl.ds(i * TILE, TILE)
        copy = pltpu.make_async_copy(schur_hbm.at[part_rows], stage_s.at[part_rows], load_sem.at[3 + i])
        copy.start()
        copies_s.append(copy)

    barrier = pltpu.get_barrier_semaphore()

    def greet(step, carry):
        pl.semaphore_signal(barrier, inc=1, device_id=(along_z(lax.rem(zc + step, GROUP)),), device_id_type=MESH)
        pl.semaphore_signal(barrier, inc=1, device_id=(along_plane(lax.rem(yx + step, GROUP)),), device_id_type=MESH)
        return carry

    lax.fori_loop(1, GROUP, greet, 0)
    present = jnp.int32(0)
    for slot in range(SLOTS):
        there = has(slot)
        present = present + jnp.where(there, 1, 0)

        @pl.when(there)
        def _(slot=slot):
            pl.semaphore_signal(barrier, inc=1, device_id=(me + OFFSETS[slot],), device_id_type=MESH)

    row_of = iface_in[...]

    @pl.loop(0, 9)
    def _(i):
        rows = pl.ds(pl.multiple_of(i * 128, 128), 128)
        ids = lax.broadcasted_iota(jnp.int32, (128, ORDER), 0) + i * 128
        scatter_m[rows, :] = jnp.where(ids == row_of, 1.0, 0.0).astype(BF16)
        across = jnp.broadcast_to(iface_in[:, rows], (128, 128)).T
        for c in range(9):
            lanes = lax.broadcasted_iota(jnp.int32, (128, 128), 1) + c * 128
            gather_m[rows, c * 128:(c + 1) * 128] = jnp.where(lanes == across, 1.0, 0.0).astype(BF16)

    phi_pad[...] = jnp.zeros_like(phi_pad)
    phi_pad[0:MODES_SUB, :] = modes_in[...]
    for c in range(9):
        piece = phi_pad[:, c * 128:(c + 1) * 128]
        phi_t[c * 128:(c + 1) * 128, :] = jnp.concatenate([piece] * 8, axis=0).T

    c_pad[...] = jnp.zeros_like(c_pad)
    c_pad[0:MODES_SUB, :] = rows_in[...]
    for half in range(2):
        @pl.loop(0, GROUP)
        def _(target, half=half):
            ids = ids_in[target, :, half * 128:(half + 1) * 128]
            ids = jnp.broadcast_to(ids, (8, 128))
            tile_id = lax.shift_right_arithmetic(ids, 7)
            lane_id = lax.bitwise_and(ids, 127)
            lane = lax.broadcasted_iota(jnp.int32, (8, 128), 1)
            sub = lax.broadcasted_iota(jnp.int32, (8, 128), 0)
            mode = lax.bitwise_and(lane, 15)
            for octet in range(2):
                total = jnp.zeros((8, 128), F32)
                for src in range(24):
                    piece = c_pad[octet * 8:(octet + 1) * 8, src * 128:(src + 1) * 128]
                    picked = jnp.take_along_axis(piece, lane_id, axis=1)
                    total = jnp.where(tile_id == src, picked, total)
                if octet == 1:
                    keep = (mode == sub + 8) & (mode >= 12) & (mode < 14)
                    total = jnp.where(keep, 1.0, total)
                c_send[target, octet * 8:(octet + 1) * 8, half * 128:(half + 1) * 128] = total

    ones = jnp.ones((ORDER, COLS), BF16)
    cnt[...] = dot(scatter_m[...], ones)

    for slot in range(SLOTS):
        @pl.when(jnp.logical_not(has(slot)))
        def _(slot=slot):
            for j in range(JUMPS):
                in_buf[j, slot * IFACE:(slot + 1) * IFACE, :] = jnp.zeros((IFACE, COLS), F32)
            for n in range(ITERS):
                cst[n, slot + 1] = jnp.zeros((BLK, COLS), F32)
    for n in range(ITERS):
        cst[n, 7] = jnp.zeros((BLK, COLS), F32)

    def load_vec(ref_to, value):
        high, low = split(value)
        ref_to[:, :COLS] = high
        ref_to[:, COLS:] = low

    def product(high_ref, low_ref, vec_ref, into):
        @pl.loop(0, ORDER // TILE)
        def _(i):
            rows = pl.ds(pl.multiple_of(i * TILE, TILE), TILE)
            total = dot(high_ref[rows, :], vec_ref[...]) + dot(low_ref[rows, :], vec_ref[...])
            into[rows, :] = fold(total)

    def scattered(jump, own):
        load_vec(vec, in_buf[jump])

        def body(i, carry):
            rows = pl.ds(pl.multiple_of(i * TILE, TILE), TILE)
            own[rows, :] = own[rows, :] - fold(dot(scatter_m[rows, :], vec[...]))
            return carry

        lax.fori_loop(0, ORDER // TILE, body, 0)

    def jump_copy(jump, slot):
        return pltpu.make_async_remote_copy(
            src_ref=out_buf.at[jump, pl.ds(slot * IFACE, IFACE)],
            dst_ref=in_buf.at[jump, pl.ds((slot ^ 1) * IFACE, IFACE)],
            send_sem=jump_send.at[jump, slot],
            recv_sem=jump_recv.at[jump, slot ^ 1],
            device_id=(me + OFFSETS[slot],),
            device_id_type=MESH,
        )

    def jump_arrival(jump, slot):
        return pltpu.make_async_remote_copy(
            src_ref=out_buf.at[jump, pl.ds(slot * IFACE, IFACE)],
            dst_ref=in_buf.at[jump, pl.ds(slot * IFACE, IFACE)],
            send_sem=jump_send.at[jump, slot],
            recv_sem=jump_recv.at[jump, slot],
            device_id=(me + OFFSETS[slot],),
            device_id_type=MESH,
        )

    def send_slot(jump, slot):
        @pl.when(has(slot))
        def _():
            jump_copy(jump, slot).start()

    def await_jump(jump):
        for slot in range(SLOTS):
            @pl.when(has(slot))
            def _(slot=slot):
                jump_arrival(jump, slot).wait_recv()

    def gather_send(jump, vec_ref):
        for first, second in PAIRS:
            rows = slice(first * IFACE, (second + 1) * IFACE)
            out_buf[jump, rows, :] = fold(dot(gather_m[rows, :], vec_ref[...]))
            send_slot(jump, first)
            send_slot(jump, second)

    load_copy.wait()
    load_vec(vec, disp[...])
    for i in range(3):
        copies_k[i].wait()
        rows = slice(i * TILE, (i + 1) * TILE)
        high, low = split(stage_k[rows, :])
        k_hi[rows, :] = high
        k_lo[rows, :] = low
    product(k_hi, k_lo, vec, disp)
    load_vec(vec, disp[...])
    pl.semaphore_wait(barrier, 2 * (GROUP - 1) + present)
    gather_send(1, vec)

    load_vec(vec2, phi_t[...])
    lane_block = lax.div(lax.broadcasted_iota(jnp.int32, (IFACE, COLS), 1), BLK)
    for slot in range(SLOTS):
        rows = slice(slot * IFACE, (slot + 1) * IFACE)
        value = fold(dot(gather_m[rows, :], vec2[...]))
        out_buf[0, rows, :] = jnp.where(lane_block == 1 + (slot ^ 1), value, 0.0)
        send_slot(0, slot)

    def send_coarse(step, carry):
        peer = lax.rem(yx + step, GROUP)
        pltpu.make_async_remote_copy(
            src_ref=c_send.at[peer], dst_ref=c_recv.at[yx], send_sem=c_ssem, recv_sem=c_rsem,
            device_id=(along_plane(peer),), device_id_type=MESH,
        ).start()
        return carry

    lax.fori_loop(1, GROUP, send_coarse, 0)
    c_recv[pl.ds(yx, 1)] = c_send[pl.ds(yx, 1)]

    for i in range(3):
        copies_s[i].wait()
        rows = slice(i * TILE, (i + 1) * TILE)
        high, low = split(stage_s[rows, :])
        s_hi[rows, :] = high
        s_lo[rows, :] = low
    high, low = split(phi_pad[...])
    both = jnp.concatenate([high, low], axis=0)
    for c in range(3):
        lanes = slice(c * TILE, (c + 1) * TILE)
        total = dot(both, s_hi[:, lanes]) + dot(both, s_lo[:, lanes])
        high, low = split(total[:BLK] + total[BLK:])
        ps[0:BLK, lanes] = high
        ps[BLK:, lanes] = low

    await_jump(0)
    lane = lax.broadcasted_iota(jnp.int32, (ORDER, COLS), 1)
    rw[...] = jnp.where(lane < BLK, phi_t[...] * cnt[...], 0.0)
    scattered(0, rw)
    load_vec(vec2, rw[...])
    product(k_hi, k_lo, vec2, rw)
    high, low = split(rw[...])
    m_hi[...] = high
    m_lo[...] = low
    vec2[:, :COLS] = high
    vec2[:, COLS:] = low
    for i in range(3):
        rows = slice(i * TILE, (i + 1) * TILE)
        total = dot(gather_m[rows, :], vec2[...])
        em_hi[rows, :] = total[:, :COLS].astype(BF16)
        em_lo[rows, :] = total[:, COLS:].astype(BF16)

    pltpu.make_async_remote_copy(
        src_ref=c_send.at[pl.ds(0, GROUP - 1)], dst_ref=c_recv.at[pl.ds(0, GROUP - 1)], send_sem=c_ssem, recv_sem=c_rsem,
        device_id=(along_plane(lax.rem(yx + 1, GROUP)),), device_id_type=MESH,
    ).wait()
    high, low = split(c_recv[...].reshape(GROUP * BLK, GROUP * BLK))
    cb_hi[...] = high
    cb_lo[...] = low

    smoothed[...] = jnp.zeros_like(smoothed)
    response[...] = jnp.zeros_like(response)
    gap[...] = jnp.zeros_like(gap)
    mult[...] = jnp.zeros_like(mult)
    coarse[...] = jnp.zeros_like(coarse)
    mult_co[...] = jnp.zeros_like(mult_co)

    await_jump(1)
    u[...] = cnt[...] * disp[...]
    scattered(1, u)

    def first_round(n):
        load_vec(vec, u[...])
        total = dot(ps[...], vec[...])
        total = fold(total[:BLK] + total[BLK:])
        upper = jnp.sum(gap[...] * u[...], axis=0, keepdims=True)
        lower = jnp.sum(u[...] * u[...], axis=0, keepdims=True)
        row = lax.broadcasted_iota(jnp.int32, (BLK, COLS), 0)
        upper = jnp.where(n == 0, 0.0, upper)
        lower = jnp.where(n == 0, 0.0, lower)
        total = jnp.where(row == 12, upper, jnp.where(row == 13, lower, total))
        pbuf[n, pl.ds(zc, 1)] = total[None]

        def send(step, carry):
            pltpu.make_async_remote_copy(
                src_ref=pbuf.at[n, zc], dst_ref=pbuf.at[n, zc], send_sem=p_ssem.at[n], recv_sem=p_rsem.at[n],
                device_id=(along_z(lax.rem(zc + step, GROUP)),), device_id_type=MESH,
            ).start()
            return carry

        lax.fori_loop(1, GROUP, send, 0)

    def whole(src, dst, ssem, rsem):
        return pltpu.make_async_remote_copy(
            src_ref=src, dst_ref=dst, send_sem=ssem, recv_sem=rsem,
            device_id=(along_z(lax.rem(zc + 1, GROUP)),), device_id_type=MESH,
        )

    def p_whole(n):
        return whole(pbuf.at[n, pl.ds(0, GROUP - 1)], pbuf.at[n, pl.ds(0, GROUP - 1)], p_ssem.at[n], p_rsem.at[n])

    def q_whole(n):
        return whole(part.at[n, pl.ds(0, GROUP - 1)], rbuf.at[n, pl.ds(0, GROUP - 1)], q_ssem.at[n], q_rsem.at[n])

    def second_round(n):
        p_whole(n).wait_recv()
        high, low = split(pbuf[n].reshape(GROUP * BLK, COLS))
        both = jnp.concatenate([high, low], axis=1)
        total = fold(dot(cb_hi[...], both) + dot(cb_lo[...], both))
        part[n] = total.reshape(GROUP, BLK, COLS)

        def send(step, carry):
            peer = lax.rem(yx + step, GROUP)
            pltpu.make_async_remote_copy(
                src_ref=part.at[n, peer], dst_ref=rbuf.at[n, yx], send_sem=q_ssem.at[n], recv_sem=q_rsem.at[n],
                device_id=(along_plane(peer),), device_id_type=MESH,
            ).start()
            return carry

        lax.fori_loop(1, GROUP, send, 0)
        rbuf[n, pl.ds(yx, 1)] = part[n, pl.ds(yx, 1)]

    def sums(n):
        q_whole(n).wait_recv()
        total = jnp.sum(rbuf[n], axis=0)
        return total, DAMPING * total[12:13] / (total[13:14] + EPSILON)

    def near_copy(n, slot, arriving):
        return pltpu.make_async_remote_copy(
            src_ref=cst.at[n, 0],
            dst_ref=cst.at[n, 1 + (slot if arriving else slot ^ 1)],
            send_sem=n_ssem.at[n, slot],
            recv_sem=n_rsem.at[n, slot if arriving else slot ^ 1],
            device_id=(me + OFFSETS[slot],),
            device_id_type=MESH,
        )

    def sweep(n, carry):
        first_round(n)
        product(s_hi, s_lo, vec, w)
        load_vec(vec2, w[...])
        gather_send(2 + 2 * n, vec2)
        second_round(n)
        await_jump(2 + 2 * n)
        lifted[...] = cnt[...] * w[...]
        scattered(2 + 2 * n, lifted)
        total, step = sums(n)
        step = jnp.where(n == 0, -1.0, step)
        total = jnp.where(lax.broadcasted_iota(jnp.int32, (BLK, COLS), 0) < MODES_SUB, total, 0.0)
        cst[n, 0] = total
        for slot in range(SLOTS):
            @pl.when(has(slot))
            def _(slot=slot):
                near_copy(n, slot, False).start()
        load_vec(vec, lifted[...])
        product(k_hi, k_lo, vec, rw)
        load_vec(vec, rw[...])
        for i in range(3):
            rows = slice(i * TILE, (i + 1) * TILE)
            gw[rows, :] = fold(dot(gather_m[rows, :], vec[...]))
        for slot in range(SLOTS):
            @pl.when(has(slot))
            def _(slot=slot):
                near_copy(n, slot, True).wait_recv()
        high, low = split(cst[n].reshape(8 * BLK, COLS))
        near = jnp.concatenate([high, low], axis=1)
        jump = 3 + 2 * n
        for first, second in PAIRS:
            rows = slice(first * IFACE, (second + 1) * IFACE)
            change = gw[rows, :] + fold(dot(em_hi[rows, :], near) + dot(em_lo[rows, :], near))
            og[rows, :] = og[rows, :] - step * change
            out_buf[jump, rows, :] = og[rows, :]
            send_slot(jump, first)
            send_slot(jump, second)
        update(step)
        gap[...] = gap[...] - step * u[...]
        smoothed[...] = smoothed[...] - step * w[...]
        coarse[...] = coarse[...] - step * total

        def body(i, inner):
            rows = pl.ds(pl.multiple_of(i * TILE, TILE), TILE)
            change = rw[rows, :] + fold(dot(m_hi[rows, :], near) + dot(m_lo[rows, :], near))
            response[rows, :] = response[rows, :] - step * change
            return inner

        lax.fori_loop(0, ORDER // TILE, body, 0)
        u[...] = cnt[...] * response[...]
        await_jump(jump)
        scattered(jump, u)
        return carry

    def update(step):
        mult[...] = mult[...] + step * smoothed[...]
        mult_co[...] = mult_co[...] + step * coarse[...]
        disp[...] = disp[...] - step * response[...]

    og[...] = jnp.zeros_like(og)
    lax.fori_loop(0, ITERS, sweep, 0)

    first_round(ITERS)
    high, low = split(jnp.where(lane < BLK, phi_t[...], 0.0))
    m_hi[...] = high
    m_lo[...] = low
    second_round(ITERS)
    total, step = sums(ITERS)
    update(step)
    out_d = pltpu.make_async_copy(disp, disp_hbm, out_sem.at[0])
    out_d.start()
    padded = jnp.concatenate([mult_co[...], jnp.zeros((COLS - BLK, COLS), F32)], axis=0)
    high, low = split(padded)
    both = jnp.concatenate([high, low], axis=1)
    mult[...] = mult[...] + fold(dot(m_hi[...], both) + dot(m_lo[...], both))
    out_m = pltpu.make_async_copy(mult, mult_hbm, out_sem.at[1])
    out_m.start()

    for slot in range(SLOTS):
        @pl.when(has(slot))
        def _(slot=slot):
            def jump_left(jump, carry):
                jump_copy(jump, slot).wait_send()
                return carry

            lax.fori_loop(0, JUMPS, jump_left, 0)

            def near_left(n, carry):
                near_copy(n, slot, False).wait_send()
                return carry

            lax.fori_loop(0, ITERS, near_left, 0)

    def rounds_left(n, carry):
        p_whole(n).wait_send()
        q_whole(n).wait_send()
        return carry

    lax.fori_loop(0, ROUNDS, rounds_left, 0)
    out_d.wait()
    out_m.wait()


def on_device(
    applied_loads,
    local_inverse,
    schur_block,
    coarse_modes,
    coarse_rows,
    mode_ids,
    neighbours,
    iface_rows,
):
    ids = mode_ids.reshape(DEVICES // 32, GROUP, 2, MODES_SUB).transpose(1, 0, 2, 3)
    ids = jnp.pad(ids, ((0, 0), (0, 0), (0, 0), (0, BLK - MODES_SUB)), constant_values=-1)
    ids = ids.reshape(GROUP, 1, GROUP * BLK)
    field = pltpu.VMEM((ORDER, COLS), F32)
    square = pltpu.VMEM((ORDER, ORDER), BF16)
    vector = pltpu.VMEM((ORDER, 2 * COLS), BF16)
    slim = pltpu.VMEM((ORDER, COLS), BF16)
    whole = pltpu.VMEM((ORDER, ORDER), F32)
    anywhere = pl.BlockSpec(memory_space=pl.ANY)
    inside = pl.BlockSpec(memory_space=pltpu.VMEM)
    dma = pltpu.SemaphoreType.DMA
    out = jax.ShapeDtypeStruct((ORDER, COLS), F32)
    return pl.pallas_call(
        kernel,
        out_shape=(out, out),
        in_specs=[anywhere, anywhere, anywhere, inside, inside, inside, inside],
        out_specs=(anywhere, anywhere),
        scratch_shapes=[
            whole, whole, square, square, square, square, square, square,
            pltpu.VMEM((JUMPS, ORDER, COLS), F32), pltpu.VMEM((JUMPS, ORDER, COLS), F32),
            vector, vector, field, field, field, field, field, field, field, field, field, field, field, field,
            field, slim, slim, slim, slim,
            pltpu.VMEM((2 * BLK, ORDER), BF16), pltpu.VMEM((BLK, ORDER), F32), pltpu.VMEM((BLK, 24 * 128), F32),
            pltpu.VMEM((GROUP, BLK, GROUP * BLK), F32), pltpu.VMEM((GROUP, BLK, GROUP * BLK), F32),
            pltpu.VMEM((GROUP * BLK, GROUP * BLK), BF16), pltpu.VMEM((GROUP * BLK, GROUP * BLK), BF16),
            pltpu.VMEM((ROUNDS, GROUP, BLK, COLS), F32), pltpu.VMEM((ROUNDS, GROUP, BLK, COLS), F32),
            pltpu.VMEM((ROUNDS, GROUP, BLK, COLS), F32), pltpu.VMEM((ITERS, 8, BLK, COLS), F32),
            pltpu.VMEM((BLK, COLS), F32), pltpu.VMEM((BLK, COLS), F32),
            dma((7,)), dma((2,)), dma((JUMPS, SLOTS)), dma((JUMPS, SLOTS)), dma, dma,
            dma((ROUNDS,)), dma((ROUNDS,)), dma((ROUNDS,)), dma((ROUNDS,)), dma((ITERS, SLOTS)), dma((ITERS, SLOTS)),
        ],
        compiler_params=pltpu.CompilerParams(
            collective_id=0, has_side_effects=True, vmem_limit_bytes=63 * 1024 * 1024
        ),
        name="dual_solve",
    )(
        applied_loads, local_inverse, schur_block, coarse_modes, coarse_rows, ids,
        iface_rows.reshape(1, ORDER),
    )


def solution(mesh):
    return jax.shard_map(
        on_device,
        mesh=mesh,
        in_specs=(
            P("sub", None),
            P("sub", None),
            P("sub", None),
            P("sub", None),
            P("sub", None),
            P(),
            P("sub", None),
            P("sub", None, None),
        ),
        out_specs=(P("sub", None), P("sub", None)),
        check_vma=False,
    )
```

```python
import jax
import jax.numpy as jnp
from jax import lax
from jax.experimental import pallas as pl
from jax.experimental.pallas import tpu as pltpu
from jax.sharding import PartitionSpec as P

ORDER = 1152
COLS = 128
MODES_SUB = 12
IFACE = 192
SLOTS = 6
ITERS = 3
DEVICES = 256
DAMPING = 0.8
EPSILON = 1e-06
OFFSETS = (1, -1, 4, -4, 16, -16)
STRIDES = (1, 4, 16)
EXTENTS = (4, 4, 16)
GROUP = 16
BLK = 16
JUMPS = 2 + 2 * ITERS
TILE = 384
F32 = jnp.float32
BF16 = jnp.bfloat16
MESH = pl.DeviceIdType.MESH
PAIRS = ((2, 3), (4, 5), (0, 1))


def dot(a, b):
    return jnp.dot(a, b, preferred_element_type=F32)


def split(value):
    high = value.astype(BF16)
    low = (value - high.astype(F32)).astype(BF16)
    return high, low


def fold(value):
    return value[:, :COLS] + value[:, COLS:]


def kernel(
    loads_hbm, inverse_hbm, schur_hbm, modes_in, rows_in, ids_in, iface_in,
    mult_hbm, disp_hbm, direction_hbm, resp_hbm, step_out,
    stage_k, stage_s, k_hi, k_lo, s_hi, s_lo, scatter_m, gather_m,
    out_buf, in_buf, vec, vec2, cnt, phi_t, u, w, lifted, rw, smoothed, response, gap, disp, mult, og,
    gw, m_hi, m_lo, em_hi, em_lo, ps, phi_pad, c_pad, c_send, c_recv, cb_hi, cb_lo,
    pbuf, part, rbuf, cst, coarse, mult_co, sums_z, sums_p,
    load_sem, out_sem, jump_send, jump_recv, c_ssem, c_rsem, p_ssem, p_rsem, q_ssem, q_rsem, n_ssem, n_rsem, last_ssem, last_rsem,
):
    me = lax.axis_index("sub")
    core = lax.rem(me, 2)
    yx = lax.rem(lax.div(me, 2), GROUP)
    zc = lax.div(me, 32) * 2 + core

    def has(slot):
        axis = slot // 2
        place = lax.rem(lax.div(me, STRIDES[axis]), EXTENTS[axis])
        return place < EXTENTS[axis] - 1 if slot % 2 == 0 else place > 0

    def along_z(index):
        return lax.div(index, 2) * 32 + yx * 2 + lax.rem(index, 2)

    def along_plane(index):
        return lax.div(me, 32) * 32 + index * 2 + core

    copies_k, copies_s = [], []
    load_copy = pltpu.make_async_copy(loads_hbm, disp, load_sem.at[6])
    load_copy.start()
    for i in range(3):
        part_rows = pl.ds(i * TILE, TILE)
        copy = pltpu.make_async_copy(inverse_hbm.at[part_rows], stage_k.at[part_rows], load_sem.at[i])
        copy.start()
        copies_k.append(copy)
    for i in range(3):
        part_rows = pl.ds(i * TILE, TILE)
        copy = pltpu.make_async_copy(schur_hbm.at[part_rows], stage_s.at[part_rows], load_sem.at[3 + i])
        copy.start()
        copies_s.append(copy)

    barrier = pltpu.get_barrier_semaphore()

    def greet(step, carry):
        pl.semaphore_signal(barrier, inc=1, device_id=(along_z(lax.rem(zc + step, GROUP)),), device_id_type=MESH)
        pl.semaphore_signal(barrier, inc=1, device_id=(along_plane(lax.rem(yx + step, GROUP)),), device_id_type=MESH)
        return carry

    lax.fori_loop(1, GROUP, greet, 0)
    present = jnp.int32(0)
    for slot in range(SLOTS):
        there = has(slot)
        present = present + jnp.where(there, 1, 0)

        @pl.when(there)
        def _(slot=slot):
            pl.semaphore_signal(barrier, inc=1, device_id=(me + OFFSETS[slot],), device_id_type=MESH)

    @pl.loop(0, 9)
    def _(i):
        rows = pl.ds(pl.multiple_of(i * 128, 128), 128)
        across = jnp.broadcast_to(iface_in[:, rows], (128, 128)).T
        for c in range(9):
            lanes = lax.broadcasted_iota(jnp.int32, (128, 128), 1) + c * 128
            gather_m[rows, c * 128:(c + 1) * 128] = jnp.where(lanes == across, 1.0, 0.0).astype(BF16)

    def load_vec(ref_to, value):
        high, low = split(value)
        ref_to[:, :COLS] = high
        ref_to[:, COLS:] = low

    def product(high_ref, low_ref, vec_ref, into):
        @pl.loop(0, ORDER // TILE)
        def _(i):
            rows = pl.ds(pl.multiple_of(i * TILE, TILE), TILE)
            total = dot(high_ref[rows, :], vec_ref[...]) + dot(low_ref[rows, :], vec_ref[...])
            into[rows, :] = fold(total)

    def jump_copy(jump, slot):
        return pltpu.make_async_remote_copy(
            src_ref=out_buf.at[jump, pl.ds(slot * IFACE, IFACE)],
            dst_ref=in_buf.at[jump, pl.ds((slot ^ 1) * IFACE, IFACE)],
            send_sem=jump_send.at[jump, slot],
            recv_sem=jump_recv.at[jump, slot ^ 1],
            device_id=(me + OFFSETS[slot],),
            device_id_type=MESH,
        )

    def jump_arrival(jump, slot):
        return pltpu.make_async_remote_copy(
            src_ref=out_buf.at[jump, pl.ds(slot * IFACE, IFACE)],
            dst_ref=in_buf.at[jump, pl.ds(slot * IFACE, IFACE)],
            send_sem=jump_send.at[jump, slot],
            recv_sem=jump_recv.at[jump, slot],
            device_id=(me + OFFSETS[slot],),
            device_id_type=MESH,
        )

    def send_slot(jump, slot):
        @pl.when(has(slot))
        def _():
            jump_copy(jump, slot).start()

    def scattered(jump, own):
        for first, second in ((0, 1), (4, 5), (2, 3)):
            for slot in (first, second):
                @pl.when(has(slot))
                def _(slot=slot):
                    jump_arrival(jump, slot).wait_recv()
            pair = slice(first * IFACE, (second + 1) * IFACE)
            high, low = split(in_buf[jump, pair, :])
            vec[pair, :COLS] = high
            vec[pair, COLS:] = low

            def body(i, carry, pair=pair):
                rows = pl.ds(pl.multiple_of(i * TILE, TILE), TILE)
                own[rows, :] = own[rows, :] - fold(dot(scatter_m[rows, pair], vec[pair, :]))
                return carry

            lax.fori_loop(0, ORDER // TILE, body, 0)

    def gather_send(jump, vec_ref):
        for first, second in PAIRS:
            rows = slice(first * IFACE, (second + 1) * IFACE)
            out_buf[jump, rows, :] = fold(dot(gather_m[rows, :], vec_ref[...]))
            send_slot(jump, first)
            send_slot(jump, second)

    load_copy.wait()
    load_vec(vec, disp[...])
    for i in range(3):
        copies_k[i].wait()
        rows = slice(i * TILE, (i + 1) * TILE)
        high, low = split(stage_k[rows, :])
        k_hi[rows, :] = high
        k_lo[rows, :] = low
        disp[rows, :] = fold(dot(high, vec[...]) + dot(low, vec[...]))
    load_vec(vec2, disp[...])
    pl.semaphore_wait(barrier, 2 * (GROUP - 1) + present)
    gather_send(1, vec2)

    for slot in range(SLOTS):
        @pl.when(jnp.logical_not(has(slot)))
        def _(slot=slot):
            for j in range(JUMPS):
                in_buf[j, slot * IFACE:(slot + 1) * IFACE, :] = jnp.zeros((IFACE, COLS), F32)
            for n in range(ITERS):
                cst[n, slot + 1] = jnp.zeros((BLK, COLS), F32)
    for n in range(ITERS):
        cst[n, 7] = jnp.zeros((BLK, COLS), F32)

    c_pad[...] = jnp.zeros_like(c_pad)
    c_pad[0:MODES_SUB, :] = rows_in[...]
    for half in range(2):
        @pl.loop(0, GROUP)
        def _(target, half=half):
            ids = ids_in[target, :, half * 128:(half + 1) * 128]
            ids = jnp.broadcast_to(ids, (8, 128))
            tile_id = lax.shift_right_arithmetic(ids, 7)
            lane_id = lax.bitwise_and(ids, 127)
            lane = lax.broadcasted_iota(jnp.int32, (8, 128), 1)
            sub = lax.broadcasted_iota(jnp.int32, (8, 128), 0)
            mode = lax.bitwise_and(lane, 15)
            for octet in range(2):
                total = jnp.zeros((8, 128), F32)
                for src in range(24):
                    piece = c_pad[octet * 8:(octet + 1) * 8, src * 128:(src + 1) * 128]
                    picked = jnp.take_along_axis(piece, lane_id, axis=1)
                    total = jnp.where(tile_id == src, picked, total)
                if octet == 1:
                    keep = (mode == sub + 8) & (mode >= 12) & (mode < 14)
                    total = jnp.where(keep, 1.0, total)
                c_send[target, octet * 8:(octet + 1) * 8, half * 128:(half + 1) * 128] = total

    def send_coarse(step, carry):
        peer = lax.rem(yx + step, GROUP)
        pltpu.make_async_remote_copy(
            src_ref=c_send.at[peer], dst_ref=c_recv.at[yx], send_sem=c_ssem, recv_sem=c_rsem,
            device_id=(along_plane(peer),), device_id_type=MESH,
        ).start()
        return carry

    lax.fori_loop(1, GROUP, send_coarse, 0)
    c_recv[pl.ds(yx, 1)] = c_send[pl.ds(yx, 1)]

    phi_pad[...] = jnp.zeros_like(phi_pad)
    phi_pad[0:MODES_SUB, :] = modes_in[...]
    for c in range(9):
        piece = phi_pad[:, c * 128:(c + 1) * 128]
        phi_t[c * 128:(c + 1) * 128, :] = jnp.concatenate([piece] * 8, axis=0).T

    row_of = iface_in[...]

    @pl.loop(0, 9)
    def _(i):
        rows = pl.ds(pl.multiple_of(i * 128, 128), 128)
        ids = lax.broadcasted_iota(jnp.int32, (128, ORDER), 0) + i * 128
        scatter_m[rows, :] = jnp.where(ids == row_of, 1.0, 0.0).astype(BF16)

    ones = jnp.ones((ORDER, COLS), BF16)
    cnt[...] = dot(scatter_m[...], ones)

    for i in range(3):
        copies_s[i].wait()
        rows = slice(i * TILE, (i + 1) * TILE)
        high, low = split(stage_s[rows, :])
        s_hi[rows, :] = high
        s_lo[rows, :] = low
    high, low = split(phi_pad[...])
    both = jnp.concatenate([high, low], axis=0)
    for c in range(3):
        lanes = slice(c * TILE, (c + 1) * TILE)
        total = dot(both, s_hi[:, lanes]) + dot(both, s_lo[:, lanes])
        high, low = split(total[:BLK] + total[BLK:])
        ps[0:BLK, lanes] = high
        ps[BLK:, lanes] = low

    load_vec(vec2, phi_t[...])
    lane_block = lax.div(lax.broadcasted_iota(jnp.int32, (IFACE, COLS), 1), BLK)
    for slot in range(SLOTS):
        rows = slice(slot * IFACE, (slot + 1) * IFACE)
        value = fold(dot(gather_m[rows, :], vec2[...]))
        out_buf[0, rows, :] = jnp.where(lane_block == 1 + (slot ^ 1), value, 0.0)

    smoothed[...] = jnp.zeros_like(smoothed)
    response[...] = jnp.zeros_like(response)
    gap[...] = jnp.zeros_like(gap)
    mult[...] = jnp.zeros_like(mult)
    og[...] = jnp.zeros_like(og)
    coarse[...] = jnp.zeros_like(coarse)
    mult_co[...] = jnp.zeros_like(mult_co)
    u[...] = cnt[...] * disp[...]
    scattered(1, u)

    def coarse_blocks():
        pltpu.make_async_remote_copy(
            src_ref=c_send.at[pl.ds(0, GROUP - 1)], dst_ref=c_recv.at[pl.ds(0, GROUP - 1)],
            send_sem=c_ssem, recv_sem=c_rsem,
            device_id=(along_plane(lax.rem(yx + 1, GROUP)),), device_id_type=MESH,
        ).wait()
        high, low = split(c_recv[...].reshape(GROUP * BLK, GROUP * BLK))
        cb_hi[...] = high
        cb_lo[...] = low

    lane = lax.broadcasted_iota(jnp.int32, (ORDER, COLS), 1)

    def coarse_response():
        rw[...] = jnp.where(lane < BLK, phi_t[...] * cnt[...], 0.0)
        scattered(0, rw)
        load_vec(vec2, rw[...])
        product(k_hi, k_lo, vec2, rw)
        high, low = split(rw[...])
        m_hi[...] = high
        m_lo[...] = low
        vec2[:, :COLS] = high
        vec2[:, COLS:] = low

        @pl.loop(0, ORDER // TILE)
        def _(i):
            rows = pl.ds(pl.multiple_of(i * TILE, TILE), TILE)
            total = dot(gather_m[rows, :], vec2[...])
            em_hi[rows, :] = total[:, :COLS].astype(BF16)
            em_lo[rows, :] = total[:, COLS:].astype(BF16)

    def first_round(n):
        load_vec(vec, u[...])
        total = dot(ps[...], vec[...])
        total = fold(total[:BLK] + total[BLK:])
        upper = jnp.sum(gap[...] * u[...], axis=0, keepdims=True)
        lower = jnp.sum(u[...] * u[...], axis=0, keepdims=True)
        row = lax.broadcasted_iota(jnp.int32, (BLK, COLS), 0)
        upper = jnp.where(n == 0, 0.0, upper)
        lower = jnp.where(n == 0, 0.0, lower)
        total = jnp.where(row == 12, upper, jnp.where(row == 13, lower, total))
        pbuf[n, pl.ds(zc, 1)] = total[None]

        def send(step, carry):
            pltpu.make_async_remote_copy(
                src_ref=pbuf.at[n, zc], dst_ref=pbuf.at[n, zc], send_sem=p_ssem.at[n], recv_sem=p_rsem.at[n],
                device_id=(along_z(lax.rem(zc + step, GROUP)),), device_id_type=MESH,
            ).start()
            return carry

        lax.fori_loop(1, GROUP, send, 0)

    def whole(src, dst, ssem, rsem):
        return pltpu.make_async_remote_copy(
            src_ref=src, dst_ref=dst, send_sem=ssem, recv_sem=rsem,
            device_id=(along_z(lax.rem(zc + 1, GROUP)),), device_id_type=MESH,
        )

    def p_whole(n):
        return whole(pbuf.at[n, pl.ds(0, GROUP - 1)], pbuf.at[n, pl.ds(0, GROUP - 1)], p_ssem.at[n], p_rsem.at[n])

    def q_whole(n):
        return whole(part.at[n, pl.ds(0, GROUP - 1)], rbuf.at[n, pl.ds(0, GROUP - 1)], q_ssem.at[n], q_rsem.at[n])

    def second_round(n):
        p_whole(n).wait_recv()
        high, low = split(pbuf[n].reshape(GROUP * BLK, COLS))
        both = jnp.concatenate([high, low], axis=1)
        total = fold(dot(cb_hi[...], both) + dot(cb_lo[...], both))
        part[n] = total.reshape(GROUP, BLK, COLS)

        def send(step, carry):
            peer = lax.rem(yx + step, GROUP)
            pltpu.make_async_remote_copy(
                src_ref=part.at[n, peer], dst_ref=rbuf.at[n, yx], send_sem=q_ssem.at[n], recv_sem=q_rsem.at[n],
                device_id=(along_plane(peer),), device_id_type=MESH,
            ).start()
            return carry

        lax.fori_loop(1, GROUP, send, 0)
        rbuf[n, pl.ds(yx, 1)] = part[n, pl.ds(yx, 1)]

    def sums(n):
        q_whole(n).wait_recv()
        total = jnp.sum(rbuf[n], axis=0)
        return total, DAMPING * total[12:13] / (total[13:14] + EPSILON)

    def near_copy(n, slot, arriving):
        return pltpu.make_async_remote_copy(
            src_ref=cst.at[n, 0],
            dst_ref=cst.at[n, 1 + (slot if arriving else slot ^ 1)],
            send_sem=n_ssem.at[n, slot],
            recv_sem=n_rsem.at[n, slot if arriving else slot ^ 1],
            device_id=(me + OFFSETS[slot],),
            device_id_type=MESH,
        )

    def sweep(n, carry):
        first_round(n)

        @pl.when(n == 0)
        def _():
            for slot in range(SLOTS):
                send_slot(0, slot)

        product(s_hi, s_lo, vec, w)
        load_vec(vec2, w[...])
        gather_send(2 + 2 * n, vec2)
        pl.when(n == 0)(coarse_blocks)
        second_round(n)
        pl.when(n == 0)(coarse_response)
        lifted[...] = cnt[...] * w[...]
        scattered(2 + 2 * n, lifted)
        total, step = sums(n)
        step = jnp.where(n == 0, -1.0, step)
        total = jnp.where(lax.broadcasted_iota(jnp.int32, (BLK, COLS), 0) < MODES_SUB, total, 0.0)
        cst[n, 0] = total
        for slot in range(SLOTS):
            @pl.when(has(slot))
            def _(slot=slot):
                near_copy(n, slot, False).start()
        load_vec(vec, lifted[...])
        product(k_hi, k_lo, vec, rw)
        load_vec(vec, rw[...])
        for i in range(3):
            rows = slice(i * TILE, (i + 1) * TILE)
            gw[rows, :] = fold(dot(gather_m[rows, :], vec[...]))
        for slot in range(SLOTS):
            @pl.when(has(slot))
            def _(slot=slot):
                near_copy(n, slot, True).wait_recv()
        high, low = split(cst[n].reshape(8 * BLK, COLS))
        near = jnp.concatenate([high, low], axis=1)
        jump = 3 + 2 * n
        for first, second in PAIRS:
            rows = slice(first * IFACE, (second + 1) * IFACE)
            change = gw[rows, :] + fold(dot(em_hi[rows, :], near) + dot(em_lo[rows, :], near))
            og[rows, :] = og[rows, :] - step * change
            out_buf[jump, rows, :] = og[rows, :]
            send_slot(jump, first)
            send_slot(jump, second)
        update(step)
        gap[...] = gap[...] - step * u[...]
        smoothed[...] = smoothed[...] - step * w[...]
        coarse[...] = coarse[...] - step * total

        def body(i, inner):
            rows = pl.ds(pl.multiple_of(i * TILE, TILE), TILE)
            change = rw[rows, :] + fold(dot(m_hi[rows, :], near) + dot(m_lo[rows, :], near))
            response[rows, :] = response[rows, :] - step * change
            return inner

        lax.fori_loop(0, ORDER // TILE, body, 0)
        u[...] = cnt[...] * response[...]
        scattered(jump, u)
        return carry

    def update(step):
        mult[...] = mult[...] + step * smoothed[...]
        mult_co[...] = mult_co[...] + step * coarse[...]
        disp[...] = disp[...] - step * response[...]

    lax.fori_loop(0, ITERS, sweep, 0)

    row = lax.broadcasted_iota(jnp.int32, (8, COLS), 0)
    upper = jnp.sum(gap[...] * u[...], axis=0, keepdims=True)
    lower = jnp.sum(u[...] * u[...], axis=0, keepdims=True)
    sums_z[pl.ds(zc, 1)] = jnp.where(row == 0, upper, jnp.where(row == 1, lower, 0.0))[None]

    def sums_copy(buffer, place, target, which):
        return pltpu.make_async_remote_copy(
            src_ref=buffer.at[place], dst_ref=buffer.at[place], send_sem=last_ssem.at[which], recv_sem=last_rsem.at[which],
            device_id=(target,), device_id_type=MESH,
        )

    def sums_whole(buffer, which):
        return whole(buffer.at[pl.ds(0, GROUP - 1)], buffer.at[pl.ds(0, GROUP - 1)], last_ssem.at[which], last_rsem.at[which])

    def send_z(turn, carry):
        sums_copy(sums_z, zc, along_z(lax.rem(zc + turn, GROUP)), 0).start()
        return carry

    lax.fori_loop(1, GROUP, send_z, 0)
    out_r = pltpu.make_async_copy(response, resp_hbm, out_sem.at[0])
    out_r.start()
    out_d = pltpu.make_async_copy(disp, disp_hbm, out_sem.at[1])
    out_d.start()
    sums_whole(sums_z, 0).wait_recv()
    sums_p[pl.ds(yx, 1)] = jnp.sum(sums_z[...], axis=0)[None]

    def send_p(turn, carry):
        sums_copy(sums_p, yx, along_plane(lax.rem(yx + turn, GROUP)), 1).start()
        return carry

    lax.fori_loop(1, GROUP, send_p, 0)

    high, low = split(jnp.where(lane < BLK, phi_t[...], 0.0))
    m_hi[...] = high
    m_lo[...] = low
    blank = jnp.zeros((COLS - BLK, COLS), F32)
    for field, few in ((mult, mult_co), (smoothed, coarse)):
        high, low = split(jnp.concatenate([few[...], blank], axis=0))
        both = jnp.concatenate([high, low], axis=1)
        field[...] = field[...] + fold(dot(m_hi[...], both) + dot(m_lo[...], both))
    out_m = pltpu.make_async_copy(mult, mult_hbm, out_sem.at[2])
    out_m.start()
    out_s = pltpu.make_async_copy(smoothed, direction_hbm, out_sem.at[3])
    out_s.start()

    for slot in range(SLOTS):
        @pl.when(has(slot))
        def _(slot=slot):
            def jump_left(jump, carry):
                jump_copy(jump, slot).wait_send()
                return carry

            lax.fori_loop(0, JUMPS, jump_left, 0)

            def near_left(n, carry):
                near_copy(n, slot, False).wait_send()
                return carry

            lax.fori_loop(0, ITERS, near_left, 0)

    def rounds_left(n, carry):
        p_whole(n).wait_send()
        q_whole(n).wait_send()
        return carry

    lax.fori_loop(0, ITERS, rounds_left, 0)
    sums_whole(sums_z, 0).wait_send()
    for copy in (out_r, out_d, out_m, out_s):
        copy.wait()
    sums_whole(sums_p, 1).wait()
    final = jnp.sum(sums_p[...], axis=0)
    step_out[...] = jnp.broadcast_to(DAMPING * final[0:1] / (final[1:2] + EPSILON), (8, COLS))


def on_device(
    applied_loads,
    local_inverse,
    schur_block,
    coarse_modes,
    coarse_rows,
    mode_ids,
    neighbours,
    iface_rows,
):
    ids = mode_ids.reshape(DEVICES // 32, GROUP, 2, MODES_SUB).transpose(1, 0, 2, 3)
    ids = jnp.pad(ids, ((0, 0), (0, 0), (0, 0), (0, BLK - MODES_SUB)), constant_values=-1)
    ids = ids.reshape(GROUP, 1, GROUP * BLK)
    field = pltpu.VMEM((ORDER, COLS), F32)
    square = pltpu.VMEM((ORDER, ORDER), BF16)
    vector = pltpu.VMEM((ORDER, 2 * COLS), BF16)
    slim = pltpu.VMEM((ORDER, COLS), BF16)
    whole = pltpu.VMEM((ORDER, ORDER), F32)
    anywhere = pl.BlockSpec(memory_space=pl.ANY)
    inside = pl.BlockSpec(memory_space=pltpu.VMEM)
    dma = pltpu.SemaphoreType.DMA
    out = jax.ShapeDtypeStruct((ORDER, COLS), F32)
    base, displaced, direction, response, step = pl.pallas_call(
        kernel,
        out_shape=(out, out, out, out, jax.ShapeDtypeStruct((8, COLS), F32)),
        in_specs=[anywhere, anywhere, anywhere, inside, inside, inside, inside],
        out_specs=(anywhere, anywhere, anywhere, anywhere, inside),
        scratch_shapes=[
            whole, whole, square, square, square, square, square, square,
            pltpu.VMEM((JUMPS, ORDER, COLS), F32), pltpu.VMEM((JUMPS, ORDER, COLS), F32),
            vector, vector, field, field, field, field, field, field, field, field, field, field, field, field,
            field, slim, slim, slim, slim,
            pltpu.VMEM((2 * BLK, ORDER), BF16), pltpu.VMEM((BLK, ORDER), F32), pltpu.VMEM((BLK, 24 * 128), F32),
            pltpu.VMEM((GROUP, BLK, GROUP * BLK), F32), pltpu.VMEM((GROUP, BLK, GROUP * BLK), F32),
            pltpu.VMEM((GROUP * BLK, GROUP * BLK), BF16), pltpu.VMEM((GROUP * BLK, GROUP * BLK), BF16),
            pltpu.VMEM((ITERS, GROUP, BLK, COLS), F32), pltpu.VMEM((ITERS, GROUP, BLK, COLS), F32),
            pltpu.VMEM((ITERS, GROUP, BLK, COLS), F32), pltpu.VMEM((ITERS, 8, BLK, COLS), F32),
            pltpu.VMEM((BLK, COLS), F32), pltpu.VMEM((BLK, COLS), F32),
            pltpu.VMEM((GROUP, 8, COLS), F32), pltpu.VMEM((GROUP, 8, COLS), F32),
            dma((7,)), dma((4,)), dma((JUMPS, SLOTS)), dma((JUMPS, SLOTS)), dma, dma,
            dma((ITERS,)), dma((ITERS,)), dma((ITERS,)), dma((ITERS,)), dma((ITERS, SLOTS)), dma((ITERS, SLOTS)),
            dma((2,)), dma((2,)),
        ],
        compiler_params=pltpu.CompilerParams(
            collective_id=0, has_side_effects=True, vmem_limit_bytes=63 * 1024 * 1024
        ),
        name="dual_solve",
    )(
        applied_loads, local_inverse, schur_block, coarse_modes, coarse_rows, ids,
        iface_rows.reshape(1, ORDER),
    )
    return base + step[0:1] * direction, displaced - step[0:1] * response


def solution(mesh):
    return jax.shard_map(
        on_device,
        mesh=mesh,
        in_specs=(
            P("sub", None),
            P("sub", None),
            P("sub", None),
            P("sub", None),
            P("sub", None),
            P(),
            P("sub", None),
            P("sub", None, None),
        ),
        out_specs=(P("sub", None), P("sub", None)),
        check_vma=False,
    )
```

```python
import jax
import jax.numpy as jnp
from jax import lax
from jax.experimental import pallas as pl
from jax.experimental.pallas import tpu as pltpu
from jax.sharding import PartitionSpec as P

ORDER = 1152
COLS = 128
MODES_SUB = 12
IFACE = 192
SLOTS = 6
ITERS = 3
DEVICES = 256
DAMPING = 0.8
EPSILON = 1e-06
OFFSETS = (1, -1, 4, -4, 16, -16)
STRIDES = (1, 4, 16)
EXTENTS = (4, 4, 16)
GROUP = 16
BLK = 16
JUMPS = 1 + 2 * ITERS
TILE = 384
F32 = jnp.float32
BF16 = jnp.bfloat16
MESH = pl.DeviceIdType.MESH
PAIRS = ((2, 3), (4, 5), (0, 1))


def dot(a, b):
    return jnp.dot(a, b, preferred_element_type=F32)


def split(value):
    high = value.astype(BF16)
    low = (value - high.astype(F32)).astype(BF16)
    return high, low


def fold(value):
    return value[:, :COLS] + value[:, COLS:]


def kernel(
    loads_hbm, inverse_hbm, schur_hbm, modes_in, rows_in, ids_in, iface_in,
    mult_hbm, disp_hbm, direction_hbm, resp_hbm, step_out,
    stage_k, stage_s, k_hi, k_lo, s_hi, s_lo, scatter_m, gather_m,
    out_buf, in_buf, vec, vec2, cnt, phi_t, u, w, lifted, rw, smoothed, response, gap, disp, mult, og,
    gw, m_hi, m_lo, em_hi, em_lo, ps, phi_pad, c_pad, c_send, c_recv, cb_hi, cb_lo,
    pbuf, part, rbuf, cst, coarse, mult_co, sums_z, sums_p, iface_row, ids_pad, phi_out, phi_near, phi_all,
    load_sem, out_sem, jump_send, jump_recv, c_ssem, c_rsem, p_ssem, p_rsem, q_ssem, q_rsem, n_ssem, n_rsem, last_ssem, last_rsem, phi_ssem, phi_rsem,
):
    me = lax.axis_index("sub")
    core = lax.rem(me, 2)
    yx = lax.rem(lax.div(me, 2), GROUP)
    layer = lax.div(me, 32)
    zc = core * 8 + layer

    def has(slot):
        axis = slot // 2
        place = lax.rem(lax.div(me, STRIDES[axis]), EXTENTS[axis])
        return place < EXTENTS[axis] - 1 if slot % 2 == 0 else place > 0

    def along_z(index):
        return lax.rem(index, 8) * 32 + yx * 2 + lax.div(index, 8)

    def along_plane(index):
        return lax.div(me, 32) * 32 + index * 2 + core

    peers_z = []
    for far in (4, 3, 5, 2, 6, 1, 7, 0):
        for other in (0, 1):
            if far or other:
                place_z = lax.rem(layer + far, 8)
                place_c = lax.rem(core + other, 2)
                peers_z.append((place_c * 8 + place_z, place_z * 32 + yx * 2 + place_c))
    peers_p = []
    place_x, place_y = lax.rem(yx, 4), lax.div(yx, 4)
    for far_y, far_x in sorted(
        ((a, b) for a in range(4) for b in range(4) if a or b), key=lambda pair: -min(pair[0], 4 - pair[0]) - min(pair[1], 4 - pair[1])
    ):
        index = lax.rem(place_y + far_y, 4) * 4 + lax.rem(place_x + far_x, 4)
        peers_p.append((index, layer * 32 + index * 2 + core))

    copies_k, copies_s = [], []
    load_copy = pltpu.make_async_copy(loads_hbm, disp, load_sem.at[6])
    load_copy.start()
    for i in range(3):
        part_rows = pl.ds(i * TILE, TILE)
        copy = pltpu.make_async_copy(inverse_hbm.at[part_rows], stage_k.at[part_rows], load_sem.at[i])
        copy.start()
        copies_k.append(copy)
    for i in range(3):
        part_rows = pl.ds(i * TILE, TILE)
        copies_s.append(pltpu.make_async_copy(schur_hbm.at[part_rows], stage_s.at[part_rows], load_sem.at[3 + i]))

    barrier = pltpu.get_barrier_semaphore()

    def greet(step, carry):
        pl.semaphore_signal(barrier, inc=1, device_id=(along_z(lax.rem(zc + step, GROUP)),), device_id_type=MESH)
        pl.semaphore_signal(barrier, inc=1, device_id=(along_plane(lax.rem(yx + step, GROUP)),), device_id_type=MESH)
        return carry

    lax.fori_loop(1, GROUP, greet, 0)
    present = jnp.int32(0)
    for slot in range(SLOTS):
        there = has(slot)
        present = present + jnp.where(there, 1, 0)

        @pl.when(there)
        def _(slot=slot):
            pl.semaphore_signal(barrier, inc=1, device_id=(me + OFFSETS[slot],), device_id_type=MESH)

    for slot in range(SLOTS):
        iface_row[0:1, slot * IFACE:(slot + 1) * IFACE] = iface_in[0, slot:slot + 1, :]

    @pl.loop(0, 9)
    def _(i):
        rows = pl.ds(pl.multiple_of(i * 128, 128), 128)
        across = jnp.broadcast_to(iface_row[0:1, rows], (128, 128)).T
        for c in range(9):
            lanes = lax.broadcasted_iota(jnp.int32, (128, 128), 1) + c * 128
            gather_m[rows, c * 128:(c + 1) * 128] = jnp.where(lanes == across, 1.0, 0.0).astype(BF16)

    def load_vec(ref_to, value):
        high, low = split(value)
        ref_to[:, :COLS] = high
        ref_to[:, COLS:] = low

    def product(high_ref, low_ref, vec_ref, into):
        @pl.loop(0, ORDER // TILE)
        def _(i):
            rows = pl.ds(pl.multiple_of(i * TILE, TILE), TILE)
            total = dot(high_ref[rows, :], vec_ref[...]) + dot(low_ref[rows, :], vec_ref[...])
            into[rows, :] = fold(total)

    def jump_copy(jump, slot):
        return pltpu.make_async_remote_copy(
            src_ref=out_buf.at[jump, pl.ds(slot * IFACE, IFACE)],
            dst_ref=in_buf.at[jump, pl.ds((slot ^ 1) * IFACE, IFACE)],
            send_sem=jump_send.at[jump, slot],
            recv_sem=jump_recv.at[jump, slot ^ 1],
            device_id=(me + OFFSETS[slot],),
            device_id_type=MESH,
        )

    def jump_arrival(jump, slot):
        return pltpu.make_async_remote_copy(
            src_ref=out_buf.at[jump, pl.ds(slot * IFACE, IFACE)],
            dst_ref=in_buf.at[jump, pl.ds(slot * IFACE, IFACE)],
            send_sem=jump_send.at[jump, slot],
            recv_sem=jump_recv.at[jump, slot],
            device_id=(me + OFFSETS[slot],),
            device_id_type=MESH,
        )

    def phi_copy(slot, arriving):
        place = slot if arriving else slot ^ 1
        return pltpu.make_async_remote_copy(
            src_ref=phi_out.at[slot],
            dst_ref=phi_near.at[place],
            send_sem=phi_ssem.at[slot],
            recv_sem=phi_rsem.at[place],
            device_id=(me + OFFSETS[slot],),
            device_id_type=MESH,
        )

    def send_slot(jump, slot):
        @pl.when(has(slot))
        def _():
            jump_copy(jump, slot).start()

    def scattered(jump, own):
        for first, second in ((0, 1), (4, 5), (2, 3)):
            for slot in (first, second):
                @pl.when(has(slot))
                def _(slot=slot):
                    jump_arrival(jump, slot).wait_recv()
            pair = slice(first * IFACE, (second + 1) * IFACE)
            high, low = split(in_buf[jump, pair, :])
            vec[pair, :COLS] = high
            vec[pair, COLS:] = low

            def body(i, carry, pair=pair):
                rows = pl.ds(pl.multiple_of(i * TILE, TILE), TILE)
                own[rows, :] = own[rows, :] - fold(dot(scatter_m[rows, pair], vec[pair, :]))
                return carry

            lax.fori_loop(0, ORDER // TILE, body, 0)

    def gather_send(jump, vec_ref):
        for first, second in PAIRS:
            rows = slice(first * IFACE, (second + 1) * IFACE)
            out_buf[jump, rows, :] = fold(dot(gather_m[rows, :], vec_ref[...]))
            send_slot(jump, first)
            send_slot(jump, second)

    load_copy.wait()
    load_vec(vec, disp[...])
    for i in range(3):
        copies_k[i].wait()
        copies_s[i].start()
        rows = slice(i * TILE, (i + 1) * TILE)
        high, low = split(stage_k[rows, :])
        k_hi[rows, :] = high
        k_lo[rows, :] = low
        disp[rows, :] = fold(dot(high, vec[...]) + dot(low, vec[...]))
    load_vec(vec2, disp[...])
    pl.semaphore_wait(barrier, 2 * (GROUP - 1) + present)
    gather_send(0, vec2)

    for slot in range(SLOTS):
        @pl.when(jnp.logical_not(has(slot)))
        def _(slot=slot):
            phi_near[slot] = jnp.zeros((BLK, GROUP * BLK), F32)
            for j in range(JUMPS):
                in_buf[j, slot * IFACE:(slot + 1) * IFACE, :] = jnp.zeros((IFACE, COLS), F32)
            for n in range(ITERS):
                cst[n, slot + 1] = jnp.zeros((BLK, COLS), F32)
    for n in range(ITERS):
        cst[n, 7] = jnp.zeros((BLK, COLS), F32)

    c_pad[...] = jnp.zeros_like(c_pad)
    c_pad[0:MODES_SUB, :] = rows_in[...]
    ids_pad[...] = jnp.full_like(ids_pad, -1)
    ids_pad[:, 0:MODES_SUB] = ids_in[...]
    for half in range(2):
        @pl.loop(0, GROUP)
        def _(target, half=half):
            ids = ids_pad[pl.ds(target * 2 + half, 8, stride=32), :]
            ids = jnp.take_along_axis(ids, lax.bitwise_and(lax.broadcasted_iota(jnp.int32, (8, 128), 1), 15), axis=1)
            mine = lax.shift_right_arithmetic(lax.broadcasted_iota(jnp.int32, (8, 128), 1), 4) == lax.broadcasted_iota(jnp.int32, (8, 128), 0)
            ids = jnp.sum(jnp.where(mine, ids, 0), axis=0, keepdims=True)
            ids = jnp.broadcast_to(ids, (8, 128))
            tile_id = lax.shift_right_arithmetic(ids, 7)
            lane_id = lax.bitwise_and(ids, 127)
            lane = lax.broadcasted_iota(jnp.int32, (8, 128), 1)
            sub = lax.broadcasted_iota(jnp.int32, (8, 128), 0)
            mode = lax.bitwise_and(lane, 15)
            for octet in range(2):
                total = jnp.zeros((8, 128), F32)
                for src in range(24):
                    piece = c_pad[octet * 8:(octet + 1) * 8, src * 128:(src + 1) * 128]
                    picked = jnp.take_along_axis(piece, lane_id, axis=1)
                    total = jnp.where(tile_id == src, picked, total)
                if octet == 1:
                    keep = (mode == sub + 8) & (mode >= 12) & (mode < 14)
                    total = jnp.where(keep, 1.0, total)
                c_send[target, octet * 8:(octet + 1) * 8, half * 128:(half + 1) * 128] = total

    def send_coarse(step, carry):
        peer = lax.rem(yx + step, GROUP)
        pltpu.make_async_remote_copy(
            src_ref=c_send.at[peer], dst_ref=c_recv.at[yx], send_sem=c_ssem, recv_sem=c_rsem,
            device_id=(along_plane(peer),), device_id_type=MESH,
        ).start()
        return carry

    lax.fori_loop(1, GROUP, send_coarse, 0)
    c_recv[pl.ds(yx, 1)] = c_send[pl.ds(yx, 1)]

    phi_pad[...] = jnp.zeros_like(phi_pad)
    phi_pad[0:MODES_SUB, :] = modes_in[...]
    for c in range(9):
        piece = phi_pad[:, c * 128:(c + 1) * 128]
        phi_t[c * 128:(c + 1) * 128, :] = jnp.concatenate([piece] * 8, axis=0).T

    row_of = iface_row[0:1, :]

    @pl.loop(0, 9)
    def _(i):
        rows = pl.ds(pl.multiple_of(i * 128, 128), 128)
        ids = lax.broadcasted_iota(jnp.int32, (128, ORDER), 0) + i * 128
        scatter_m[rows, :] = jnp.where(ids == row_of, 1.0, 0.0).astype(BF16)

    ones = jnp.ones((ORDER, COLS), BF16)
    cnt[...] = dot(scatter_m[...], ones)

    for i in range(3):
        copies_s[i].wait()
        rows = slice(i * TILE, (i + 1) * TILE)
        high, low = split(stage_s[rows, :])
        s_hi[rows, :] = high
        s_lo[rows, :] = low
    high, low = split(phi_pad[...])
    both = jnp.concatenate([high, low], axis=0)
    for c in range(3):
        lanes = slice(c * TILE, (c + 1) * TILE)
        total = dot(both, s_hi[:, lanes]) + dot(both, s_lo[:, lanes])
        high, low = split(total[:BLK] + total[BLK:])
        ps[0:BLK, lanes] = high
        ps[BLK:, lanes] = low

    total = dot(both, scatter_m[...])
    total = total[:BLK] + total[BLK:]
    for slot in range(SLOTS):
        phi_out[slot, :, 0:IFACE] = total[:, slot * IFACE:(slot + 1) * IFACE]

        @pl.when(has(slot))
        def _(slot=slot):
            phi_copy(slot, False).start()

    smoothed[...] = jnp.zeros_like(smoothed)
    response[...] = jnp.zeros_like(response)
    gap[...] = jnp.zeros_like(gap)
    mult[...] = jnp.zeros_like(mult)
    og[...] = jnp.zeros_like(og)
    coarse[...] = jnp.zeros_like(coarse)
    mult_co[...] = jnp.zeros_like(mult_co)
    u[...] = cnt[...] * disp[...]
    scattered(0, u)

    def coarse_blocks():
        pltpu.make_async_remote_copy(
            src_ref=c_send.at[pl.ds(0, GROUP - 1)], dst_ref=c_recv.at[pl.ds(0, GROUP - 1)],
            send_sem=c_ssem, recv_sem=c_rsem,
            device_id=(along_plane(lax.rem(yx + 1, GROUP)),), device_id_type=MESH,
        ).wait()
        high, low = split(c_recv[...].reshape(GROUP * BLK, GROUP * BLK))
        cb_hi[...] = high
        cb_lo[...] = low

    lane = lax.broadcasted_iota(jnp.int32, (ORDER, COLS), 1)

    def coarse_response():
        phi_all[...] = jnp.zeros_like(phi_all)
        for slot in range(SLOTS):
            @pl.when(has(slot))
            def _(slot=slot):
                phi_copy(slot, True).wait_recv()

            phi_all[(slot + 1) * BLK:(slot + 2) * BLK, slot * IFACE:(slot + 1) * IFACE] = phi_near[slot, :, 0:IFACE]
        high, low = split(phi_all[...])
        both = jnp.concatenate([high, low], axis=0)
        rw[...] = jnp.where(lane < BLK, phi_t[...] * cnt[...], 0.0)
        for i in range(3):
            rows = slice(i * TILE, (i + 1) * TILE)
            taken = lax.dot_general(scatter_m[rows, :], both, (((1,), (1,)), ((), ())), preferred_element_type=F32)
            rw[rows, :] = rw[rows, :] - fold(taken)
        load_vec(vec2, rw[...])
        product(k_hi, k_lo, vec2, rw)
        high, low = split(rw[...])
        m_hi[...] = high
        m_lo[...] = low
        vec2[:, :COLS] = high
        vec2[:, COLS:] = low

        @pl.loop(0, ORDER // TILE)
        def _(i):
            rows = pl.ds(pl.multiple_of(i * TILE, TILE), TILE)
            total = dot(gather_m[rows, :], vec2[...])
            em_hi[rows, :] = total[:, :COLS].astype(BF16)
            em_lo[rows, :] = total[:, COLS:].astype(BF16)

    def first_round(n):
        load_vec(vec, u[...])
        total = dot(ps[...], vec[...])
        total = fold(total[:BLK] + total[BLK:])
        upper = jnp.sum(gap[...] * u[...], axis=0, keepdims=True)
        lower = jnp.sum(u[...] * u[...], axis=0, keepdims=True)
        row = lax.broadcasted_iota(jnp.int32, (BLK, COLS), 0)
        upper = jnp.where(n == 0, 0.0, upper)
        lower = jnp.where(n == 0, 0.0, lower)
        total = jnp.where(row == 12, upper, jnp.where(row == 13, lower, total))
        pbuf[n, pl.ds(zc, 1)] = total[None]

        for _, device in peers_z:
            pltpu.make_async_remote_copy(
                src_ref=pbuf.at[n, zc], dst_ref=pbuf.at[n, zc], send_sem=p_ssem.at[n], recv_sem=p_rsem.at[n],
                device_id=(device,), device_id_type=MESH,
            ).start()

    def whole(src, dst, ssem, rsem):
        return pltpu.make_async_remote_copy(
            src_ref=src, dst_ref=dst, send_sem=ssem, recv_sem=rsem,
            device_id=(along_z(lax.rem(zc + 1, GROUP)),), device_id_type=MESH,
        )

    def p_whole(n):
        return whole(pbuf.at[n, pl.ds(0, GROUP - 1)], pbuf.at[n, pl.ds(0, GROUP - 1)], p_ssem.at[n], p_rsem.at[n])

    def q_whole(n):
        return whole(part.at[n, pl.ds(0, GROUP - 1)], rbuf.at[n, pl.ds(0, GROUP - 1)], q_ssem.at[n], q_rsem.at[n])

    def second_round(n):
        p_whole(n).wait_recv()
        high, low = split(pbuf[n].reshape(GROUP * BLK, COLS))
        both = jnp.concatenate([high, low], axis=1)
        total = fold(dot(cb_hi[...], both) + dot(cb_lo[...], both))
        part[n] = total.reshape(GROUP, BLK, COLS)

        for peer, device in peers_p:
            pltpu.make_async_remote_copy(
                src_ref=part.at[n, peer], dst_ref=rbuf.at[n, yx], send_sem=q_ssem.at[n], recv_sem=q_rsem.at[n],
                device_id=(device,), device_id_type=MESH,
            ).start()
        rbuf[n, pl.ds(yx, 1)] = part[n, pl.ds(yx, 1)]

    def sums(n):
        q_whole(n).wait_recv()
        total = jnp.sum(rbuf[n], axis=0)
        return total, DAMPING * total[12:13] / (total[13:14] + EPSILON)

    def near_copy(n, slot, arriving):
        return pltpu.make_async_remote_copy(
            src_ref=cst.at[n, 0],
            dst_ref=cst.at[n, 1 + (slot if arriving else slot ^ 1)],
            send_sem=n_ssem.at[n, slot],
            recv_sem=n_rsem.at[n, slot if arriving else slot ^ 1],
            device_id=(me + OFFSETS[slot],),
            device_id_type=MESH,
        )

    def sweep(n, carry):
        first_round(n)

        product(s_hi, s_lo, vec, w)
        load_vec(vec2, w[...])
        gather_send(1 + 2 * n, vec2)
        pl.when(n == 0)(coarse_blocks)
        second_round(n)
        pl.when(n == 0)(coarse_response)
        lifted[...] = cnt[...] * w[...]
        scattered(1 + 2 * n, lifted)
        total, step = sums(n)
        step = jnp.where(n == 0, -1.0, step)
        total = jnp.where(lax.broadcasted_iota(jnp.int32, (BLK, COLS), 0) < MODES_SUB, total, 0.0)
        cst[n, 0] = total
        for slot in range(SLOTS):
            @pl.when(has(slot))
            def _(slot=slot):
                near_copy(n, slot, False).start()
        load_vec(vec, lifted[...])
        product(k_hi, k_lo, vec, rw)
        load_vec(vec, rw[...])
        for i in range(3):
            rows = slice(i * TILE, (i + 1) * TILE)
            gw[rows, :] = fold(dot(gather_m[rows, :], vec[...]))
        for slot in range(SLOTS):
            @pl.when(has(slot))
            def _(slot=slot):
                near_copy(n, slot, True).wait_recv()
        high, low = split(cst[n].reshape(8 * BLK, COLS))
        near = jnp.concatenate([high, low], axis=1)
        jump = 2 + 2 * n
        for first, second in PAIRS:
            rows = slice(first * IFACE, (second + 1) * IFACE)
            change = gw[rows, :] + fold(dot(em_hi[rows, :], near) + dot(em_lo[rows, :], near))
            og[rows, :] = og[rows, :] - step * change
            out_buf[jump, rows, :] = og[rows, :]
            send_slot(jump, first)
            send_slot(jump, second)
        update(step)
        gap[...] = gap[...] - step * u[...]
        smoothed[...] = smoothed[...] - step * w[...]
        coarse[...] = coarse[...] - step * total

        def body(i, inner):
            rows = pl.ds(pl.multiple_of(i * TILE, TILE), TILE)
            change = rw[rows, :] + fold(dot(m_hi[rows, :], near) + dot(m_lo[rows, :], near))
            response[rows, :] = response[rows, :] - step * change
            return inner

        lax.fori_loop(0, ORDER // TILE, body, 0)
        u[...] = cnt[...] * response[...]
        scattered(jump, u)
        return carry

    def update(step):
        mult[...] = mult[...] + step * smoothed[...]
        mult_co[...] = mult_co[...] + step * coarse[...]
        disp[...] = disp[...] - step * response[...]

    lax.fori_loop(0, ITERS, sweep, 0)

    row = lax.broadcasted_iota(jnp.int32, (8, COLS), 0)
    upper = jnp.sum(gap[...] * u[...], axis=0, keepdims=True)
    lower = jnp.sum(u[...] * u[...], axis=0, keepdims=True)
    sums_z[pl.ds(zc, 1)] = jnp.where(row == 0, upper, jnp.where(row == 1, lower, 0.0))[None]

    def sums_copy(buffer, place, target, which):
        return pltpu.make_async_remote_copy(
            src_ref=buffer.at[place], dst_ref=buffer.at[place], send_sem=last_ssem.at[which], recv_sem=last_rsem.at[which],
            device_id=(target,), device_id_type=MESH,
        )

    def sums_whole(buffer, which):
        return whole(buffer.at[pl.ds(0, GROUP - 1)], buffer.at[pl.ds(0, GROUP - 1)], last_ssem.at[which], last_rsem.at[which])

    for _, device in peers_z:
        sums_copy(sums_z, zc, device, 0).start()
    out_r = pltpu.make_async_copy(response, resp_hbm, out_sem.at[0])
    out_r.start()
    out_d = pltpu.make_async_copy(disp, disp_hbm, out_sem.at[1])
    out_d.start()
    sums_whole(sums_z, 0).wait_recv()
    sums_p[pl.ds(yx, 1)] = jnp.sum(sums_z[...], axis=0)[None]

    for _, device in peers_p:
        sums_copy(sums_p, yx, device, 1).start()

    high, low = split(jnp.where(lane < BLK, phi_t[...], 0.0))
    m_hi[...] = high
    m_lo[...] = low
    blank = jnp.zeros((COLS - BLK, COLS), F32)
    for field, few in ((mult, mult_co), (smoothed, coarse)):
        high, low = split(jnp.concatenate([few[...], blank], axis=0))
        both = jnp.concatenate([high, low], axis=1)
        field[...] = field[...] + fold(dot(m_hi[...], both) + dot(m_lo[...], both))
    out_m = pltpu.make_async_copy(mult, mult_hbm, out_sem.at[2])
    out_m.start()
    out_s = pltpu.make_async_copy(smoothed, direction_hbm, out_sem.at[3])
    out_s.start()

    for slot in range(SLOTS):
        @pl.when(has(slot))
        def _(slot=slot):
            def jump_left(jump, carry):
                jump_copy(jump, slot).wait_send()
                return carry

            phi_copy(slot, False).wait_send()
            lax.fori_loop(0, JUMPS, jump_left, 0)

            def near_left(n, carry):
                near_copy(n, slot, False).wait_send()
                return carry

            lax.fori_loop(0, ITERS, near_left, 0)

    def rounds_left(n, carry):
        p_whole(n).wait_send()
        q_whole(n).wait_send()
        return carry

    lax.fori_loop(0, ITERS, rounds_left, 0)
    sums_whole(sums_z, 0).wait_send()
    for copy in (out_r, out_d, out_m, out_s):
        copy.wait()
    sums_whole(sums_p, 1).wait()
    final = jnp.sum(sums_p[...], axis=0)
    step_out[...] = DAMPING * final[0:1] / (final[1:2] + EPSILON)


def on_device(
    applied_loads,
    local_inverse,
    schur_block,
    coarse_modes,
    coarse_rows,
    mode_ids,
    neighbours,
    iface_rows,
):
    field = pltpu.VMEM((ORDER, COLS), F32)
    square = pltpu.VMEM((ORDER, ORDER), BF16)
    vector = pltpu.VMEM((ORDER, 2 * COLS), BF16)
    slim = pltpu.VMEM((ORDER, COLS), BF16)
    whole = pltpu.VMEM((ORDER, ORDER), F32)
    anywhere = pl.BlockSpec(memory_space=pl.ANY)
    inside = pl.BlockSpec(memory_space=pltpu.VMEM)
    dma = pltpu.SemaphoreType.DMA
    out = jax.ShapeDtypeStruct((ORDER, COLS), F32)
    base, displaced, direction, response, step = pl.pallas_call(
        kernel,
        out_shape=(out, out, out, out, jax.ShapeDtypeStruct((1, COLS), F32)),
        in_specs=[anywhere, anywhere, anywhere, inside, inside, inside, inside],
        out_specs=(anywhere, anywhere, anywhere, anywhere, inside),
        scratch_shapes=[
            whole, whole, square, square, square, square, square, square,
            pltpu.VMEM((JUMPS, ORDER, COLS), F32), pltpu.VMEM((JUMPS, ORDER, COLS), F32),
            vector, vector, field, field, field, field, field, field, field, field, field, field, field, field,
            field, slim, slim, slim, slim,
            pltpu.VMEM((2 * BLK, ORDER), BF16), pltpu.VMEM((BLK, ORDER), F32), pltpu.VMEM((BLK, 24 * 128), F32),
            pltpu.VMEM((GROUP, BLK, GROUP * BLK), F32), pltpu.VMEM((GROUP, BLK, GROUP * BLK), F32),
            pltpu.VMEM((GROUP * BLK, GROUP * BLK), BF16), pltpu.VMEM((GROUP * BLK, GROUP * BLK), BF16),
            pltpu.VMEM((ITERS, GROUP, BLK, COLS), F32), pltpu.VMEM((ITERS, GROUP, BLK, COLS), F32),
            pltpu.VMEM((ITERS, GROUP, BLK, COLS), F32), pltpu.VMEM((ITERS, 8, BLK, COLS), F32),
            pltpu.VMEM((BLK, COLS), F32), pltpu.VMEM((BLK, COLS), F32),
            pltpu.VMEM((GROUP, 8, COLS), F32), pltpu.VMEM((GROUP, 8, COLS), F32),
            pltpu.VMEM((8, ORDER), jnp.int32), pltpu.VMEM((DEVICES, 128), jnp.int32),
            pltpu.VMEM((SLOTS, BLK, GROUP * BLK), F32), pltpu.VMEM((SLOTS, BLK, GROUP * BLK), F32), pltpu.VMEM((COLS, ORDER), F32),
            dma((7,)), dma((4,)), dma((JUMPS, SLOTS)), dma((JUMPS, SLOTS)), dma, dma,
            dma((ITERS,)), dma((ITERS,)), dma((ITERS,)), dma((ITERS,)), dma((ITERS, SLOTS)), dma((ITERS, SLOTS)),
            dma((2,)), dma((2,)), dma((SLOTS,)), dma((SLOTS,)),
        ],
        compiler_params=pltpu.CompilerParams(
            collective_id=0, has_side_effects=True, vmem_limit_bytes=63 * 1024 * 1024
        ),
        name="dual_solve",
    )(
        applied_loads, local_inverse, schur_block, coarse_modes, coarse_rows, mode_ids, iface_rows,
    )
    return base + step * direction, displaced - step * response


def solution(mesh):
    return jax.shard_map(
        on_device,
        mesh=mesh,
        in_specs=(
            P("sub", None),
            P("sub", None),
            P("sub", None),
            P("sub", None),
            P("sub", None),
            P(),
            P("sub", None),
            P("sub", None, None),
        ),
        out_specs=(P("sub", None), P("sub", None)),
        check_vma=False,
    )
```
